32 devices in a mesh: dp: 16 (over z, x, core), mp: 2 (over y).
Axes of the slice: x: 2, y: 2, z: 4, core: 2. Of those that a mesh axis runs over, the one named last changes fastest.
Arguments:
- tokens: bfloat16 [64, 1024, 1024], P('dp', 'mp'), may hold values from -6 to 6
- w_qkv: bfloat16 [3, 1024, 1024], P(None, 'dp', 'mp'), may hold values from -0.1875 to 0.1875
- w_out: bfloat16 [1024, 1024], P('mp', 'dp'), may hold values from -1 to 1
- w_up: bfloat16 [1024, 4096], P('dp', 'mp'), may hold values from -0.1875 to 0.1875
- w_down: bfloat16 [4096, 1024], P('mp', 'dp'), may hold values from -0.09375 to 0.09375
- ln_gain: bfloat16 [2, 1024], P(None, 'dp'), may hold values from 0.5 to 1.5
- ln_shift: bfloat16 [2, 1024], P(None, 'dp'), may hold values from -2 to 2
- doc_lens: int32 [64, 8], P('dp'), may hold values from 1 to 256, 1024 in all within a row
- cotangent: bfloat16 [64, 1024, 1024], P('dp', 'mp'), may hold values from -6 to 6
Outputs:
- output: bfloat16 [64, 1024, 1024], P('dp', 'mp')
- tokens_grad: float32 [64, 1024, 1024], P('dp', 'mp')
- w_qkv_grad: float32 [3, 1024, 1024], P(None, 'dp', 'mp')
- w_out_grad: float32 [1024, 1024], P('mp', 'dp')
- w_up_grad: float32 [1024, 4096], P('dp', 'mp')
- w_down_grad: float32 [4096, 1024], P('mp', 'dp')
- ln_gain_grad: float32 [2, 1024], P(None, 'dp')
- ln_shift_grad: float32 [2, 1024], P(None, 'dp')
The draws below stay inside these ranges and needn't reach their ends.
Inputs may be any that keep to these rules, and one draw needn't show every extreme that they name: `doc_lens`: each row's 8 document lengths add up to 1024, and the longest of every row is exactly 256.
All inputs are finite; a program needn't handle non-finite values.
Results may differ from the reference program's by a relative error of at most 0.018.
Values may be sent and summed in bfloat16 or wider, within the bound.
No kernel may reach another device: no remote copies, remote signals or barrier semaphores. Data moves between devices by JAX's collectives and lax.ppermute only.
A program may use at most 448 MiB of HBM per device.

```python
import math
import jax
import jax.numpy as jnp
import numpy as np
from jax import lax

D = 1024
HEADS = 16
HEAD_DIM = 64
FF = 4096
BLOCK = 64
NDOC = 8
LEN = 1024
MOST = 256
BATCH = 64


def block_levels(stream_key, shape, shards, low, top_value):
    level, own = 1.0, jax.random.fold_in(stream_key, 6)
    for position, blocks in shards:
        steps = jnp.exp(jax.random.uniform(jax.random.fold_in(own, position), (blocks,), jnp.float32, low / len(shards), top_value / len(shards)))
        level = level * jnp.repeat(steps, shape[position] // blocks).reshape([-1 if axis == position else 1 for axis in range(len(shape))])
    return level


def split_up(number_of, total, limit, lean):
    loads = [(1 << 20) // math.isqrt(standing ** lean) + 1 for standing in range(2, number_of + 1)]
    rest, given = total - limit - (number_of - 1), [1] * (number_of - 1)
    while rest > 0:
        free = [i for i in range(number_of - 1) if given[i] < limit]
        whole, remaining = sum([loads[i] for i in free]), rest
        for i in free:
            extra = min(limit - given[i], max(1, remaining * loads[i] // whole), rest)
            given[i] = given[i] + extra
            rest = rest - extra
    return np.array([limit] + given)


def uneven(rng, count, total, reach, lean):
    if count == 2:
        one = jax.random.randint(rng, (), max(1, total - reach), min(reach, total - 1) + 1)
        return jnp.stack([one, total - one])
    sizes = jnp.asarray(split_up(count, total, reach, lean), jnp.int32)
    twos = (count - 1) // 2
    giver, sink = sizes[1:1 + 2 * twos:2], sizes[2:2 + 2 * twos:2]
    slack = jnp.minimum(giver - 1, reach - sink)
    passed = jax.random.randint(jax.random.fold_in(rng, 1), (twos,), 0, 1 << 20) % (slack + 1)
    sizes = sizes.at[1:1 + 2 * twos:2].set(giver - passed).at[2:2 + 2 * twos:2].set(sink + passed)
    return sizes[jax.random.permutation(jax.random.fold_in(rng, 2), count)]


def scatter_about(key, dims, scale, most, shards=(), kind=jnp.bfloat16):
    loudness = block_levels(key, dims, shards, -0.22, 0.18) if shards else 1.0
    values = jax.random.normal(key, dims, jnp.float32) * scale * loudness
    return jnp.minimum(jnp.maximum(values, -most), most).astype(kind)


def setup_inputs(seed: int = 0) -> dict:
    streams_of = jax.random.split(jax.random.key(seed), 10)
    return {
        "tokens": scatter_about(streams_of[0], (BATCH, LEN, D), 1.0, 6.0, ((0, 16), (1, 2))),
        "w_qkv": scatter_about(streams_of[1], (3, D, D), D ** -0.5, 0.1875, ((1, 16), (2, 2))),
        "w_out": scatter_about(streams_of[2], (D, D), (D // 32) ** -0.5, 1.0, ((0, 2), (1, 16))),
        "w_up": scatter_about(streams_of[3], (D, FF), D ** -0.5, 0.1875, ((0, 16), (1, 2))),
        "w_down": scatter_about(streams_of[4], (FF, D), FF ** -0.5, 0.09375, ((0, 2), (1, 16))),
        "ln_gain": jnp.clip(1.0 + 0.1 * jax.random.normal(streams_of[5], (2, D), jnp.float32), 0.5, 1.5).astype(jnp.bfloat16),
        "ln_shift": scatter_about(streams_of[6], (2, D), 0.3, 2.0, ((1, 16),)),
        "doc_lens": jax.vmap(lambda own: uneven(own, NDOC, LEN, MOST, 2))(jax.random.split(streams_of[7], BATCH)).reshape((BATCH, NDOC)).astype(jnp.int32),
        "cotangent": scatter_about(streams_of[8], (BATCH, LEN, D), 1.0, 6.0, ((0, 16), (1, 2))),
    }


@jax.custom_vjp
def low(v):
    return lax.optimization_barrier(v.astype(jnp.bfloat16)).astype(jnp.float32)

@jax.custom_vjp
def low_back(v):
    return v

def low_keep(v):
    return (low(v), None)

def low_pass(kept, grad):
    return (grad,)

def back_keep(v):
    return (v, None)

def back_low(kept, grad):
    return (low(grad),)
low.defvjp(low_keep, low_pass)
low_back.defvjp(back_keep, back_low)
layer_eps = 1e-05
highest = lax.Precision.HIGHEST

def layer_norm(values, scale_row, shift_row):
    average = lax.optimization_barrier(jnp.mean(values, -1, keepdims=True))
    centered = values - average
    variance = lax.optimization_barrier(jnp.mean(centered * centered, -1, keepdims=True))
    return centered * lax.rsqrt(variance + layer_eps) * scale_row + shift_row

def gelu_curve(values):
    return jax.nn.gelu(values, approximate=True)

def doc_layout(lengths, seq_len, block_len):
    lengths = lengths.astype(jnp.int32)
    starts = (jnp.cumsum(lengths) - lengths).astype(jnp.int32)
    places = jnp.arange(seq_len, dtype=jnp.int32)
    member = ((places[:, None] >= starts[None, :]) & (places[:, None] < (starts + lengths)[None, :])).astype(jnp.int32)
    labels = jnp.arange(lengths.shape[0], dtype=jnp.int32)
    doc_index = lax.optimization_barrier(jnp.sum(member * labels[None, :], 1)).astype(jnp.int32)
    offset = (places - lax.optimization_barrier(jnp.sum(member * starts[None, :], 1))).astype(jnp.int32)
    extent = lax.optimization_barrier(jnp.sum(member * lengths[None, :], 1)).astype(jnp.int32)
    angles = 0.5 * math.pi * offset.astype(jnp.float32) / extent.astype(jnp.float32)
    blocks = seq_len // block_len
    doc_ids = doc_index.reshape(blocks, block_len)
    last_doc = doc_ids[:, block_len - 1]
    before = jnp.concatenate([jnp.full((1,), -1, jnp.int32), last_doc[:blocks - 1]])
    inside = jnp.arange(block_len, dtype=jnp.int32)
    causal = inside[:, None] >= inside[None, :]
    same_doc = ((doc_ids[:, :, None] == doc_ids[:, None, :]) & causal[None]).astype(jnp.float32)
    usable = (doc_ids == before[:, None]).astype(jnp.float32)
    tail_mask = (doc_ids == last_doc[:, None]).astype(jnp.float32)
    carried = (before == last_doc).astype(jnp.float32)
    cos_wave = jnp.cos(angles).reshape(blocks, block_len, 1, 1)
    sine_wave = jnp.sin(angles).reshape(blocks, block_len, 1, 1)
    return (cos_wave, sine_wave, same_doc, usable, tail_mask, carried)

def featurize(raw, cos_wave, sine_wave):
    positive = jax.nn.relu(raw)
    return low(jnp.concatenate([positive * cos_wave, positive * sine_wave], -1))

def attend(q_feat, k_feat, v_low, layout):
    cos_wave, sine_wave, same_doc, usable, tail_mask, carried = layout
    raw_scores = jnp.einsum('ntaf,njaf->natj', q_feat, k_feat, precision=highest) * same_doc[:, None]
    scores = low_back(raw_scores)
    scores_low = low(scores)
    within = jnp.einsum('natj,njae->ntae', scores_low, v_low, precision=highest)
    totals = jnp.transpose(lax.optimization_barrier(jnp.sum(scores, 3)), (0, 2, 1))
    tail_keys = k_feat * tail_mask[:, :, None, None]
    summary = low_back(jnp.einsum('njaf,njae->nafe', tail_keys, v_low, precision=highest))
    key_sums = lax.optimization_barrier(jnp.sum(tail_keys, 1))

    def advance(carried_in, entries):
        memory, norm_memory = carried_in
        block_term, block_sum, keep_flag = entries
        return ((keep_flag * memory + block_term, keep_flag * norm_memory + block_sum), (memory, norm_memory))
    start_state = (jnp.zeros(summary.shape[1:], jnp.float32), jnp.zeros(key_sums.shape[1:], jnp.float32))
    unused, (states, norm_states) = lax.scan(advance, start_state, (summary, key_sums, carried))
    across = jnp.einsum('ntaf,nafe->ntae', q_feat, low(states), precision=highest)
    across_norm = lax.optimization_barrier(jnp.sum(q_feat * norm_states[:, None], 3))
    numer = low_back(within + usable[:, :, None, None] * across)
    denom = 1.0 + totals + usable[:, :, None] * across_norm
    return numer / denom[..., None]

def row_layer(row_tokens, lengths, w_qkv, w_out, w_up, w_down, ln_gain, ln_shift):
    seq_len = row_tokens.shape[0]
    blocks = seq_len // BLOCK
    layout = doc_layout(lengths, seq_len, BLOCK)
    projected = low_back(jnp.einsum('td,kdc->ktc', row_tokens, w_qkv, precision=highest))
    projected = projected.reshape(3, blocks, BLOCK, HEADS, HEAD_DIM)
    q_feat = featurize(projected[0], layout[0], layout[1])
    k_feat = featurize(projected[1], layout[0], layout[1])
    v_low = low(projected[2])
    attended = attend(q_feat, k_feat, v_low, layout)
    out_low = low(attended.reshape(seq_len, D))
    attn = low_back(jnp.dot(out_low, w_out, precision=highest))
    normed = layer_norm(row_tokens + attn, ln_gain[0], ln_shift[0])
    upper = low_back(jnp.dot(low(normed), w_up, precision=highest))
    active = low(gelu_curve(upper))
    ffn = low_back(jnp.dot(active, w_down, precision=highest))
    return layer_norm(normed + ffn, ln_gain[1], ln_shift[1])

def forward(tokens, w_qkv, w_out, w_up, w_down, ln_gain, ln_shift, doc_lens):

    def one_row(pair):
        return row_layer(pair[0], pair[1], w_qkv, w_out, w_up, w_down, ln_gain, ln_shift)
    return lax.map(jax.checkpoint(one_row), (tokens, doc_lens))

def reference(tokens, w_qkv, w_out, w_up, w_down, ln_gain, ln_shift, doc_lens, cotangent):

    def layer_fn(x_in, qkv_in, out_in, up_in, down_in, gain_in, shift_in):
        return forward(x_in, qkv_in, out_in, up_in, down_in, gain_in, shift_in, doc_lens)
    result, pullback = jax.vjp(layer_fn, tokens.astype(jnp.float32), w_qkv.astype(jnp.float32), w_out.astype(jnp.float32), w_up.astype(jnp.float32), w_down.astype(jnp.float32), ln_gain.astype(jnp.float32), ln_shift.astype(jnp.float32))
    grads = pullback(cotangent.astype(jnp.float32))
    return (result.astype(jnp.bfloat16), grads[0], grads[1], grads[2], grads[3], grads[4], grads[5], grads[6])
```

```python
import math
from functools import partial

import jax
import jax.numpy as jnp
from jax import lax
from jax.experimental import pallas as pl
from jax.experimental.pallas import tpu as pltpu
from jax.sharding import PartitionSpec as P

HEAD_DIM = 64
BLOCK = 64


layer_eps = 1e-05


def layer_norm(values, scale_row, shift_row):
    average = jnp.mean(values, -1, keepdims=True)
    centered = values - average
    variance = jnp.mean(centered * centered, -1, keepdims=True)
    return centered * lax.rsqrt(variance + layer_eps) * scale_row + shift_row


def gelu_curve(values):
    return jax.nn.gelu(values, approximate=True)


def doc_layout(lengths, seq_len, block_len):
    starts = jnp.cumsum(lengths) - lengths
    places = jnp.arange(seq_len, dtype=jnp.int32)
    member = (
        (places[:, None] >= starts[None, :]) & (places[:, None] < (starts + lengths)[None, :])
    ).astype(jnp.int32)
    labels = jnp.arange(lengths.shape[0], dtype=jnp.int32)
    doc_index = jnp.sum(member * labels[None, :], 1)
    offset = places - jnp.sum(member * starts[None, :], 1)
    extent = jnp.sum(member * lengths[None, :], 1)
    angles = 0.5 * math.pi * offset.astype(jnp.float32) / extent.astype(jnp.float32)
    blocks = seq_len // block_len
    doc_ids = doc_index.reshape(blocks, block_len)
    last_doc = doc_ids[:, block_len - 1]
    before = jnp.concatenate([jnp.full((1,), -1, jnp.int32), last_doc[: blocks - 1]])
    inside = jnp.arange(block_len, dtype=jnp.int32)
    causal = inside[:, None] >= inside[None, :]
    same_doc = ((doc_ids[:, :, None] == doc_ids[:, None, :]) & causal[None]).astype(jnp.float32)
    usable = (doc_ids == before[:, None]).astype(jnp.float32)
    tail_mask = (doc_ids == last_doc[:, None]).astype(jnp.float32)
    carried = (before == last_doc).astype(jnp.float32)
    cos_wave = jnp.cos(angles).reshape(blocks, block_len, 1, 1)
    sine_wave = jnp.sin(angles).reshape(blocks, block_len, 1, 1)
    return (cos_wave, sine_wave, same_doc, usable, tail_mask, carried)


def featurize(raw, cos_wave, sine_wave):
    positive = jnp.maximum(raw, 0.0)
    return jnp.concatenate([positive * cos_wave, positive * sine_wave], -1).astype(jnp.bfloat16)


def unfeature(grad_feat, raw, cos_wave, sine_wave):
    head_size = raw.shape[-1]
    folded = grad_feat[..., :head_size] * cos_wave + grad_feat[..., head_size:] * sine_wave
    return folded * (raw > 0.0).astype(jnp.float32)


def attend_forward(q_feat, k_feat, v_low, layout):
    cos_wave, sine_wave, same_doc, usable, tail_mask, carried = layout
    scores = (
        jnp.einsum("ntaf,njaf->natj", q_feat, k_feat, preferred_element_type=jnp.float32)
        * same_doc[:, None]
    )
    scores_low = scores.astype(jnp.bfloat16)
    within = jnp.einsum("natj,njae->ntae", scores_low, v_low, preferred_element_type=jnp.float32)
    totals = jnp.transpose(jnp.sum(scores, 3), (0, 2, 1))
    tail_keys = k_feat * tail_mask[:, :, None, None].astype(jnp.bfloat16)
    summary = jnp.einsum("njaf,njae->nafe", tail_keys, v_low, preferred_element_type=jnp.float32)
    key_sums = jnp.sum(tail_keys.astype(jnp.float32), 1)

    def advance(carried_in, entries):
        memory, norm_memory = carried_in
        block_term, block_sum, keep_flag = entries
        return (
            (keep_flag * memory + block_term, keep_flag * norm_memory + block_sum),
            (memory, norm_memory),
        )

    start_state = (
        jnp.zeros(summary.shape[1:], jnp.float32),
        jnp.zeros(key_sums.shape[1:], jnp.float32),
    )
    unused, (states, norm_states) = lax.scan(advance, start_state, (summary, key_sums, carried))
    states_low = states.astype(jnp.bfloat16)
    across = jnp.einsum("ntaf,nafe->ntae", q_feat, states_low, preferred_element_type=jnp.float32)
    across_norm = jnp.sum(q_feat.astype(jnp.float32) * norm_states[:, None], 3)
    numer = within + usable[:, :, None, None] * across
    denom = 1.0 + totals + usable[:, :, None] * across_norm
    output = numer / denom[..., None]
    return (output, (scores_low, states_low, norm_states, denom, output))


def attend_backward(grad_out, q_feat, k_feat, v_low, layout, saved):
    cos_wave, sine_wave, same_doc, usable, tail_mask, carried = layout
    scores_low, states_low, norm_states, denom, output = saved
    grad_numer = (grad_out / denom[..., None]).astype(jnp.bfloat16)
    grad_denom = -jnp.sum(grad_out * output, 3) / denom
    grad_scores = jnp.einsum(
        "ntae,njae->natj", grad_numer, v_low, preferred_element_type=jnp.float32
    )
    grad_scores = grad_scores + jnp.transpose(grad_denom, (0, 2, 1))[..., None]
    grad_scores = (grad_scores * same_doc[:, None]).astype(jnp.bfloat16)
    grad_query = jnp.einsum(
        "natj,njaf->ntaf", grad_scores, k_feat, preferred_element_type=jnp.float32
    )
    grad_key = jnp.einsum(
        "natj,ntaf->njaf", grad_scores, q_feat, preferred_element_type=jnp.float32
    )
    grad_value = jnp.einsum(
        "natj,ntae->njae", scores_low, grad_numer, preferred_element_type=jnp.float32
    )
    used_grad = grad_numer * usable[:, :, None, None].astype(jnp.bfloat16)
    used_denom = usable[:, :, None] * grad_denom
    grad_query = grad_query + jnp.einsum(
        "ntae,nafe->ntaf", used_grad, states_low, preferred_element_type=jnp.float32
    )
    grad_query = grad_query + used_denom[..., None] * norm_states[:, None]
    grad_states = jnp.einsum(
        "ntaf,ntae->nafe", q_feat, used_grad, preferred_element_type=jnp.float32
    )
    grad_norms = jnp.sum(used_denom[..., None] * q_feat.astype(jnp.float32), 1)

    def retreat(later, entries):
        later_state, later_norm = later
        block_term, block_norm, keep_flag = entries
        return (
            (block_term + keep_flag * later_state, block_norm + keep_flag * later_norm),
            (later_state, later_norm),
        )

    start_state = (
        jnp.zeros(grad_states.shape[1:], jnp.float32),
        jnp.zeros(grad_norms.shape[1:], jnp.float32),
    )
    unused, (grad_summary, grad_sums) = lax.scan(
        retreat, start_state, (grad_states, grad_norms, carried), reverse=True
    )
    summary_low = grad_summary.astype(jnp.bfloat16)
    tail_keys = k_feat * tail_mask[:, :, None, None].astype(jnp.bfloat16)
    from_state = jnp.einsum(
        "njae,nafe->njaf", v_low, summary_low, preferred_element_type=jnp.float32
    )
    grad_key = grad_key + tail_mask[:, :, None, None] * (from_state + grad_sums[:, None])
    grad_value = grad_value + jnp.einsum(
        "njaf,nafe->njae", tail_keys, summary_low, preferred_element_type=jnp.float32
    )
    return (grad_query, grad_key, grad_value)


def split_body(tokens, w_qkv, w_out, w_up, w_down, ln_gain, ln_shift, doc_lens, cotangent):
    groups = lax.axis_size("mp")
    per_dev = tokens.shape[1]
    seq_len = per_dev * groups
    blocks = seq_len // BLOCK
    width_local = w_qkv.shape[2]
    head_local = width_local // HEAD_DIM
    qkv_full, out_full, up_full, down_full, gain_full, shift_full = (
        lax.all_gather(w_qkv, "dp", axis=1, tiled=True),
        lax.all_gather(w_out, "dp", axis=1, tiled=True),
        lax.all_gather(w_up, "dp", axis=0, tiled=True),
        lax.all_gather(w_down, "dp", axis=1, tiled=True),
        lax.all_gather(ln_gain, "dp", axis=1, tiled=True),
        lax.all_gather(ln_shift, "dp", axis=1, tiled=True),
    )
    gains = gain_full.astype(jnp.float32)
    shifts = shift_full.astype(jnp.float32)
    acc_qkv = jnp.zeros(qkv_full.shape, jnp.float32)
    acc_out = jnp.zeros(out_full.shape, jnp.float32)
    acc_up = jnp.zeros(up_full.shape, jnp.float32)
    acc_down = jnp.zeros(down_full.shape, jnp.float32)
    acc_gain = jnp.zeros(gains.shape, jnp.float32)
    acc_shift = jnp.zeros(shifts.shape, jnp.float32)
    results = []
    input_grads = []
    for batch_row in range(tokens.shape[0]):
        x_local = tokens[batch_row]
        x_whole = lax.all_gather(x_local, "mp", axis=0, tiled=True)
        layout = doc_layout(doc_lens[batch_row], seq_len, BLOCK)
        cos_wave, sine_wave = (layout[0], layout[1])
        projected = jnp.einsum("td,kdc->ktc", x_whole, qkv_full, preferred_element_type=jnp.float32)
        projected = projected.reshape(3, blocks, BLOCK, head_local, HEAD_DIM)
        q_feat = featurize(projected[0], cos_wave, sine_wave)
        k_feat = featurize(projected[1], cos_wave, sine_wave)
        v_low = projected[2].astype(jnp.bfloat16)
        attended, saved = attend_forward(q_feat, k_feat, v_low, layout)
        out_low = attended.reshape(seq_len, width_local).astype(jnp.bfloat16)
        attn = lax.psum_scatter(
            jnp.dot(out_low, out_full, preferred_element_type=jnp.float32),
            "mp",
            scatter_dimension=0,
            tiled=True,
        )
        normed, first_back = jax.vjp(
            layer_norm, x_local.astype(jnp.float32) + attn, gains[0], shifts[0]
        )
        normed_low = normed.astype(jnp.bfloat16)
        normed_whole = lax.all_gather(normed_low, "mp", axis=0, tiled=True)
        upper = jnp.dot(normed_whole, up_full, preferred_element_type=jnp.float32)
        active, gelu_back = jax.vjp(gelu_curve, upper)
        active_low = active.astype(jnp.bfloat16)
        ffn = lax.psum_scatter(
            jnp.dot(active_low, down_full, preferred_element_type=jnp.float32),
            "mp",
            scatter_dimension=0,
            tiled=True,
        )
        result, second_back = jax.vjp(layer_norm, normed + ffn, gains[1], shifts[1])
        results.append(result.astype(jnp.bfloat16))
        grad_second, gain_second, shift_second = second_back(
            cotangent[batch_row].astype(jnp.float32)
        )
        second_low = grad_second.astype(jnp.bfloat16)
        second_whole = lax.all_gather(second_low, "mp", axis=0, tiled=True)
        grad_active = jnp.einsum(
            "td,fd->tf", second_whole, down_full, preferred_element_type=jnp.float32
        )
        acc_down = acc_down + jnp.einsum(
            "tf,td->fd", active_low, second_whole, preferred_element_type=jnp.float32
        )
        (grad_upper,) = gelu_back(grad_active)
        upper_low = grad_upper.astype(jnp.bfloat16)
        acc_up = acc_up + jnp.einsum(
            "td,tf->df", normed_whole, upper_low, preferred_element_type=jnp.float32
        )
        back_ffn = lax.psum_scatter(
            jnp.einsum("tf,df->td", upper_low, up_full, preferred_element_type=jnp.float32),
            "mp",
            scatter_dimension=0,
            tiled=True,
        )
        grad_resid, gain_first, shift_first = first_back(grad_second + back_ffn)
        acc_gain = acc_gain + jnp.stack([gain_first, gain_second])
        acc_shift = acc_shift + jnp.stack([shift_first, shift_second])
        resid_whole = lax.all_gather(grad_resid.astype(jnp.bfloat16), "mp", axis=0, tiled=True)
        grad_attended = jnp.einsum(
            "td,cd->tc", resid_whole, out_full, preferred_element_type=jnp.float32
        )
        acc_out = acc_out + jnp.einsum(
            "tc,td->cd", out_low, resid_whole, preferred_element_type=jnp.float32
        )
        grad_query, grad_key, grad_value = attend_backward(
            grad_attended.reshape(blocks, BLOCK, head_local, HEAD_DIM),
            q_feat,
            k_feat,
            v_low,
            layout,
            saved,
        )
        grad_proj = jnp.stack(
            [
                unfeature(grad_query, projected[0], cos_wave, sine_wave),
                unfeature(grad_key, projected[1], cos_wave, sine_wave),
                grad_value,
            ]
        )
        grad_proj = grad_proj.reshape(3, seq_len, width_local).astype(jnp.bfloat16)
        acc_qkv = acc_qkv + jnp.einsum(
            "td,ktc->kdc", x_whole, grad_proj, preferred_element_type=jnp.float32
        )
        back_input = lax.psum_scatter(
            jnp.einsum(
                "ktc,kdc->td", grad_proj, qkv_full, preferred_element_type=jnp.float32
            ).astype(jnp.bfloat16),
            "mp",
            scatter_dimension=0,
            tiled=True,
        ).astype(jnp.float32)
        input_grads.append(grad_resid + back_input)
    qkv_grad, out_grad, up_grad, down_grad, gain_part, shift_part = (
        lax.psum_scatter(
            acc_qkv.astype(jnp.bfloat16), "dp", scatter_dimension=1, tiled=True
        ).astype(jnp.float32),
        lax.psum_scatter(
            acc_out.astype(jnp.bfloat16), "dp", scatter_dimension=1, tiled=True
        ).astype(jnp.float32),
        lax.psum_scatter(acc_up.astype(jnp.bfloat16), "dp", scatter_dimension=0, tiled=True).astype(
            jnp.float32
        ),
        lax.psum_scatter(
            acc_down.astype(jnp.bfloat16), "dp", scatter_dimension=1, tiled=True
        ).astype(jnp.float32),
        lax.psum_scatter(
            acc_gain.astype(jnp.bfloat16), "dp", scatter_dimension=1, tiled=True
        ).astype(jnp.float32),
        lax.psum_scatter(
            acc_shift.astype(jnp.bfloat16), "dp", scatter_dimension=1, tiled=True
        ).astype(jnp.float32),
    )
    gain_grad, shift_grad = lax.psum((gain_part, shift_part), "mp")
    return (
        jnp.stack(results),
        jnp.stack(input_grads),
        qkv_grad,
        out_grad,
        up_grad,
        down_grad,
        gain_grad,
        shift_grad,
    )


TILE = 256


def tables(lengths, seq_len):
    starts = jnp.cumsum(lengths, -1) - lengths
    places = jnp.arange(seq_len, dtype=jnp.int32)
    member = (
        (places[None, :, None] >= starts[:, None, :])
        & (places[None, :, None] < (starts + lengths)[:, None, :])
    ).astype(jnp.int32)
    first = jnp.sum(member * starts[:, None, :], 2)
    extent = jnp.sum(member * lengths[:, None, :], 2)
    angles = 0.5 * math.pi * (places[None] - first).astype(jnp.float32) / extent.astype(jnp.float32)
    rows = jnp.stack([jnp.cos(angles), jnp.sin(angles), first.astype(jnp.float32)], 1)
    rows = jnp.pad(rows, ((0, 0), (0, 5), (0, 0)))
    return rows, jnp.transpose(rows, (0, 2, 1))


def lane_ids(shape):
    return lax.broadcasted_iota(jnp.int32, shape, len(shape) - 1)


def attend_kernel(parts, tiles_each, me_ref, rows_ref, cols_ref, qkv_ref, out_ref, den_ref, mask_ref):
    me = me_ref[0]
    tiles = parts * tiles_each

    @pl.when(pl.program_id(1) == 0)
    def _():
        for i in range(tiles):
            own = pl.ds(i * TILE, TILE)
            cos_t, sin_t = cols_ref[own, 0:1], cols_ref[own, 1:2]
            first_t = cols_ref[own, 2:3].astype(jnp.int32)
            t_ids = lax.broadcasted_iota(jnp.int32, (TILE, TILE), 0) + i * TILE
            for back in range(2 if i else 1):
                keys = pl.ds((i - back) * TILE, TILE)
                j_ids = lax.broadcasted_iota(jnp.int32, (TILE, TILE), 1) + (i - back) * TILE
                wave = cos_t * rows_ref[0:1, keys] + sin_t * rows_ref[1:2, keys]
                mask_ref[i, back] = jnp.where((j_ids <= t_ids) & (j_ids >= first_t), wave, 0.0)

    lanes = lane_ids((TILE, 128))
    left = lanes < HEAD_DIM
    zero = jnp.zeros((), jnp.bfloat16)
    one = jnp.ones((), jnp.bfloat16)

    def tile_of(i, which):
        part = lax.rem(i // tiles_each + parts - me, parts)
        row = (i % tiles_each) * TILE
        return qkv_ref[part, pl.ds(row, TILE), pl.ds(which * 128, 128)]

    for i in range(tiles):
        q_pair = tile_of(i, 0)
        sums = []
        for head in range(2):
            here = left if head == 0 else ~left
            q_one = jnp.where(here, q_pair, zero)
            acc = None
            for back in range(2 if i else 1):
                scores = lax.dot_general(
                    q_one, tile_of(i - back, 1), (((1,), (1,)), ((), ())),
                    preferred_element_type=jnp.float32,
                )
                weights = (scores * mask_ref[i, back]).astype(jnp.bfloat16)
                v_one = jnp.where(here, tile_of(i - back, 2), one)
                part = jnp.dot(weights, v_one, preferred_element_type=jnp.float32)
                acc = part if acc is None else acc + part
            sums.append(acc)
        numer = jnp.where(left, sums[0], sums[1])
        denom = 1.0 + pltpu.roll(jnp.where(left, sums[1], sums[0]), HEAD_DIM, 1)
        part = lax.rem(i // tiles_each + parts - me, parts)
        rows = pl.ds((i % tiles_each) * TILE, TILE)
        out_ref[part, rows, :] = (numer / denom).astype(jnp.bfloat16)
        den_ref[part, rows, :] = denom


def attend_back_kernel(
    parts, tiles_each, me_ref, rows_ref, cols_ref, qkv_ref, out_ref, den_ref, dout_ref, grad_ref, mask_ref, dk_ref, dv_ref
):
    me = me_ref[0]
    tiles = parts * tiles_each

    @pl.when(pl.program_id(1) == 0)
    def _():
        for i in range(tiles):
            own = pl.ds(i * TILE, TILE)
            cos_t, sin_t = rows_ref[0:1, own], rows_ref[1:2, own]
            first_t = rows_ref[2:3, own].astype(jnp.int32)
            t_ids = lax.broadcasted_iota(jnp.int32, (TILE, TILE), 1) + i * TILE
            for back in range(2 if i else 1):
                keys = pl.ds((i - back) * TILE, TILE)
                j_ids = lax.broadcasted_iota(jnp.int32, (TILE, TILE), 0) + (i - back) * TILE
                wave = cols_ref[keys, 0:1] * cos_t + cols_ref[keys, 1:2] * sin_t
                mask_ref[i, back] = jnp.where((j_ids <= t_ids) & (j_ids >= first_t), wave, 0.0)

    lanes = lane_ids((TILE, 128))
    left = lanes < HEAD_DIM
    zero = jnp.zeros((), jnp.bfloat16)
    one = jnp.ones((), jnp.bfloat16)
    swap = (
        (lax.broadcasted_iota(jnp.int32, (128, 128), 0) < HEAD_DIM)
        != (lax.broadcasted_iota(jnp.int32, (128, 128), 1) < HEAD_DIM)
    ).astype(jnp.bfloat16)
    nt = (((1,), (1,)), ((), ()))

    def place(i):
        return lax.rem(i // tiles_each + parts - me, parts), pl.ds((i % tiles_each) * TILE, TILE)

    def tile_of(i, which):
        part, rows = place(i)
        return qkv_ref[part, rows, pl.ds(which * 128, 128)]

    def finish(i):
        part, rows = place(i)
        k_pair = tile_of(i, 1)
        grad_ref[part, rows, pl.ds(128, 128)] = jnp.where(k_pair > 0, dk_ref[i], 0.0).astype(
            jnp.bfloat16
        )
        grad_ref[part, rows, pl.ds(256, 128)] = dv_ref[i].astype(jnp.bfloat16)

    for i in range(tiles):
        part, rows = place(i)
        q_pair = tile_of(i, 0)
        denom = den_ref[part, rows, :]
        dout = dout_ref[part, rows, :].astype(jnp.float32)
        inverse = 1.0 / denom
        dnum = (dout * inverse).astype(jnp.bfloat16)
        product = dout * inverse * out_ref[part, rows, :].astype(jnp.float32)
        high = product.astype(jnp.bfloat16)
        low = (product - high.astype(jnp.float32)).astype(jnp.bfloat16)
        dden = -(
            jnp.dot(high, swap, preferred_element_type=jnp.float32)
            + jnp.dot(low, swap, preferred_element_type=jnp.float32)
        )
        dden_high = dden.astype(jnp.bfloat16)
        dden_low = (dden - dden_high.astype(jnp.float32)).astype(jnp.bfloat16)
        heads = []
        for head in range(2):
            here = left if head == 0 else ~left
            at = HEAD_DIM if head == 0 else 0
            spare = jnp.where(lanes == at, dden_high, jnp.where(lanes == at + 1, dden_low, zero))
            ones = jnp.where((lanes == at) | (lanes == at + 1), one, zero)
            heads.append(
                (
                    here,
                    ones,
                    jnp.where(here, q_pair, zero),
                    jnp.where(here, dnum, zero),
                    jnp.where(here, dnum, spare),
                )
            )
        dq_cols = [None, None]
        for back in range(2 if i else 1):
            j = i - back
            k_pair, v_pair = tile_of(j, 1), tile_of(j, 2)
            k_cols = jnp.transpose(k_pair.astype(jnp.float32)).astype(jnp.bfloat16)
            mask = mask_ref[i, back]
            dk_part, dv_part = None, None
            for head in range(2):
                here, ones, q_one, dnum_one, dnum_more = heads[head]
                scores = lax.dot_general(k_pair, q_one, nt, preferred_element_type=jnp.float32)
                weights = (scores * mask).astype(jnp.bfloat16)
                v_one = jnp.where(here, v_pair, ones)
                dscores = lax.dot_general(v_one, dnum_more, nt, preferred_element_type=jnp.float32)
                dscores = (dscores * mask).astype(jnp.bfloat16)
                dv_one = jnp.dot(weights, dnum_one, preferred_element_type=jnp.float32)
                dk_one = jnp.dot(dscores, q_one, preferred_element_type=jnp.float32)
                dv_part = dv_one if dv_part is None else dv_part + dv_one
                dk_part = dk_one if dk_part is None else dk_part + dk_one
                dq_one = jnp.dot(
                    k_cols[head * HEAD_DIM : (head + 1) * HEAD_DIM],
                    dscores,
                    preferred_element_type=jnp.float32,
                )
                dq_cols[head] = dq_one if dq_cols[head] is None else dq_cols[head] + dq_one
            if back == 0:
                dk_ref[i] = dk_part
                dv_ref[i] = dv_part
            else:
                dk_ref[j] = dk_ref[j] + dk_part
                dv_ref[j] = dv_ref[j] + dv_part
                finish(j)
        dq = jnp.transpose(jnp.concatenate(dq_cols, 0))
        grad_ref[part, rows, pl.ds(0, 128)] = jnp.where(q_pair > 0, dq, 0.0).astype(jnp.bfloat16)
    finish(tiles - 1)


def attention(me, rows, cols, qkv):
    parts, seqs, per_dev, width = qkv.shape
    pairs = width // 384
    seq_len = parts * per_dev
    tiles_each = per_dev // TILE
    block = lambda w: pl.BlockSpec((parts, None, per_dev, w), lambda s, p, m: (0, s, 0, p))
    return pl.pallas_call(
        partial(attend_kernel, parts, tiles_each),
        name="attend",
        grid_spec=pltpu.PrefetchScalarGridSpec(
            num_scalar_prefetch=1,
            grid=(seqs, pairs),
            in_specs=[
                pl.BlockSpec((None, 8, seq_len), lambda s, p, m: (s, 0, 0)),
                pl.BlockSpec((None, seq_len, 8), lambda s, p, m: (s, 0, 0)),
                block(384),
            ],
            out_specs=[block(128), block(128)],
            scratch_shapes=[pltpu.VMEM((parts * tiles_each, 2, TILE, TILE), jnp.float32)],
        ),
        out_shape=[
            jax.ShapeDtypeStruct((parts, seqs, per_dev, pairs * 128), jnp.bfloat16),
            jax.ShapeDtypeStruct((parts, seqs, per_dev, pairs * 128), jnp.float32),
        ],
        compiler_params=pltpu.CompilerParams(dimension_semantics=("arbitrary", "arbitrary")),
    )(me, rows, cols, qkv)


def attention_back(me, rows, cols, qkv, out, den, dout):
    parts, seqs, per_dev, width = qkv.shape
    pairs = width // 384
    seq_len = parts * per_dev
    tiles = seq_len // TILE
    block = lambda w: pl.BlockSpec((parts, None, per_dev, w), lambda s, p, m: (0, s, 0, p))
    return pl.pallas_call(
        partial(attend_back_kernel, parts, per_dev // TILE),
        name="attend_back",
        grid_spec=pltpu.PrefetchScalarGridSpec(
            num_scalar_prefetch=1,
            grid=(seqs, pairs),
            in_specs=[
                pl.BlockSpec((None, 8, seq_len), lambda s, p, m: (s, 0, 0)),
                pl.BlockSpec((None, seq_len, 8), lambda s, p, m: (s, 0, 0)),
                block(384),
                block(128),
                block(128),
                block(128),
            ],
            out_specs=block(384),
            scratch_shapes=[
                pltpu.VMEM((tiles, 2, TILE, TILE), jnp.float32),
                pltpu.VMEM((tiles, TILE, 128), jnp.float32),
                pltpu.VMEM((tiles, TILE, 128), jnp.float32),
            ],
        ),
        out_shape=jax.ShapeDtypeStruct(qkv.shape, jnp.bfloat16),
        compiler_params=pltpu.CompilerParams(dimension_semantics=("arbitrary", "arbitrary")),
    )(me, rows, cols, qkv, out, den, dout)


def shift_parts(value, step):
    groups = lax.axis_size("mp")
    return lax.ppermute(value, "mp", [(i, (i + step) % groups) for i in range(groups)])


def rows_of(array, owner, count):
    return lax.dynamic_slice_in_dim(array, owner * count, count, 0)


def bring(array, me, count):
    groups = lax.axis_size("mp")
    pieces = [rows_of(array, me, count)]
    for step in range(1, groups):
        owner = lax.rem(me + groups - step, groups)
        pieces.append(shift_parts(rows_of(array, owner, count), groups - step))
    return pieces


def give_back(pieces, me):
    groups = len(pieces)
    if groups == 1:
        return pieces[0]
    count = pieces[0].shape[0]
    full = jnp.concatenate([pieces[0]] * groups, 0)
    for step in range(1, groups):
        came = shift_parts(pieces[step], step).astype(full.dtype)
        owner = lax.rem(me + groups - step, groups)
        full = lax.dynamic_update_slice_in_dim(full, came, owner * count, 0)
    return full


def norm_parts(values):
    average = jnp.mean(values, -1, keepdims=True)
    centered = values - average
    scale = lax.rsqrt(jnp.mean(centered * centered, -1, keepdims=True) + layer_eps)
    return centered * scale, scale


def norm_back(grad, unit, scale, gain):
    inner = grad * gain
    first = jnp.mean(inner, -1, keepdims=True)
    second = jnp.mean(inner * unit, -1, keepdims=True)
    return scale * (inner - first - unit * second)


def dot_nn(a, b):
    return jnp.dot(a, b, preferred_element_type=jnp.float32)


def dot_nt(a, b):
    return lax.dot_general(a, b, (((1,), (1,)), ((), ())), preferred_element_type=jnp.float32)


def dot_tn(a, b):
    return lax.dot_general(a, b, (((0,), (0,)), ((), ())), preferred_element_type=jnp.float32)


def body(tokens, w_qkv, w_out, w_up, w_down, ln_gain, ln_shift, doc_lens, cotangent):
    groups = lax.axis_size("mp")
    n_rows, per_dev, width = tokens.shape
    seq_len = per_dev * groups
    cols_each = w_qkv.shape[2]
    if n_rows % groups or per_dev % TILE or cols_each % 128:
        return split_body(
            tokens, w_qkv, w_out, w_up, w_down, ln_gain, ln_shift, doc_lens, cotangent
        )
    low = jnp.bfloat16
    me = lax.axis_index("mp")
    me_arr = me.reshape(1).astype(jnp.int32)
    count = n_rows // groups
    pairs = cols_each // 128
    local = w_qkv.shape[1]
    ff = w_up.shape[1]
    axes = ("mp", "dp")
    own_qkv = jnp.transpose(w_qkv.reshape(3, local, pairs, 128), (1, 2, 0, 3))
    own_qkv = own_qkv.reshape(local, 3 * cols_each)
    norms = jnp.pad(jnp.concatenate([ln_gain, ln_shift], 0).T, ((0, 0), (0, 124)))
    own_rest = jnp.concatenate([w_out.T, w_up, w_down.T, norms], 1)
    full_qkv = lax.all_gather(own_qkv, axes, axis=0, tiled=True).reshape(groups, width, -1)
    full_rest = lax.all_gather(own_rest, axes, axis=0, tiled=True).reshape(groups, width, -1)
    o1, o2, o3 = cols_each, cols_each + ff, cols_each + 2 * ff
    out_t = [full_rest[h, :, :o1] for h in range(groups)]
    up_w = [full_rest[h, :, o1:o2] for h in range(groups)]
    down_t = [full_rest[h, :, o2:o3] for h in range(groups)]
    vectors = full_rest[0, :, o3 : o3 + 4].T.astype(jnp.float32)
    gains, shifts = vectors[:2], vectors[2:]
    halves = range(groups)

    x_all = jnp.stack(bring(tokens, me, count))
    x2 = x_all.reshape(-1, width)
    seed_all = jnp.stack(bring(cotangent, me, count)).reshape(-1, width)
    rows, cols = tables(rows_of(doc_lens, me, count), seq_len)
    shape4 = (groups, count, per_dev)

    is_relu = lax.broadcasted_iota(jnp.int32, (1, 3 * cols_each), 1) % 384 < 256
    floor = jnp.where(is_relu, 0.0, -jnp.inf)
    qkv = [
        jnp.maximum(dot_nn(x2, full_qkv[h]), floor).astype(low).reshape(*shape4, -1)
        for h in halves
    ]
    outs, dens = [], []
    for h in halves:
        out_h, den_h = attention(me_arr, rows, cols, qkv[h])
        outs.append(out_h)
        dens.append(den_h)
    outs2 = [o.reshape(-1, cols_each) for o in outs]
    attn = sum(dot_nt(outs2[h], out_t[h]) for h in halves)
    unit0, scale0 = norm_parts(x2.astype(jnp.float32) + attn)
    normed = unit0 * gains[0] + shifts[0]
    normed_low = normed.astype(low)
    upper = [dot_nn(normed_low, up_w[h]) for h in halves]
    active, slopes = [], []
    for h in halves:
        act, back = jax.vjp(gelu_curve, upper[h])
        active.append(act.astype(low))
        slopes.append(back(jnp.ones_like(act))[0].astype(low))
    ffn = sum(dot_nt(active[h], down_t[h]) for h in halves)
    unit1, scale1 = norm_parts(normed + ffn)
    result = (unit1 * gains[1] + shifts[1]).astype(low).reshape(*shape4, width)
    result = give_back([result[k] for k in range(groups)], me)

    seed = seed_all.astype(jnp.float32)
    g2 = norm_back(seed, unit1, scale1, gains[1])
    gain1 = jnp.sum(seed * unit1, 0)
    shift1 = jnp.sum(seed, 0)
    g2_low = g2.astype(low)
    down_grad = [dot_tn(g2_low, active[h]).astype(low) for h in halves]
    dup = [
        (dot_nn(g2_low, down_t[h]) * slopes[h].astype(jnp.float32)).astype(low) for h in halves
    ]
    up_grad = [dot_tn(normed_low, dup[h]).astype(low) for h in halves]
    dnormed = g2 + sum(dot_nt(dup[h], up_w[h]) for h in halves)
    g1 = norm_back(dnormed, unit0, scale0, gains[0])
    gain0 = jnp.sum(dnormed * unit0, 0)
    shift0 = jnp.sum(dnormed, 0)
    g1_low = g1.astype(low)
    out_grad = [dot_tn(g1_low, outs2[h]).astype(low) for h in halves]
    norm_grads = jnp.stack([gain0, gain1, shift0, shift1], 1)
    norm_grads = jnp.pad(norm_grads, ((0, 0), (0, 124))).astype(low)
    ffn_grads = jnp.stack(
        [jnp.concatenate([up_grad[h], down_grad[h]], 1) for h in halves]
    ).reshape(groups * width, -1)
    ffn_part = lax.psum_scatter(ffn_grads, axes, scatter_dimension=0, tiled=True)
    dqkv = []
    for h in halves:
        dout = dot_nn(g1_low, out_t[h]).astype(low).reshape(*shape4, -1)
        grads = attention_back(me_arr, rows, cols, qkv[h], outs[h], dens[h], dout)
        dqkv.append(grads.reshape(-1, 3 * cols_each))
    tokens_grad = g1 + sum(dot_nt(dqkv[h], full_qkv[h]) for h in halves)
    tokens_grad = tokens_grad.reshape(*shape4, width)
    qkv_grad = [dot_tn(x2, dqkv[h]).astype(low) for h in halves]
    last_grads = jnp.stack(
        [jnp.concatenate([qkv_grad[h], out_grad[h], norm_grads], 1) for h in halves]
    ).reshape(groups * width, -1)
    last_part = lax.psum_scatter(last_grads, axes, scatter_dimension=0, tiled=True)
    tokens_grad = give_back(
        [tokens_grad[0]] + [tokens_grad[k].astype(low) for k in range(1, groups)], me
    )

    f32 = jnp.float32
    grad_qkv = last_part[:, : 3 * cols_each].astype(f32).reshape(local, pairs, 3, 128)
    grad_qkv = jnp.transpose(grad_qkv, (2, 0, 1, 3)).reshape(3, local, cols_each)
    grad_out = last_part[:, 3 * cols_each : 4 * cols_each].astype(f32).T
    grad_norm = last_part[:, 4 * cols_each : 4 * cols_each + 4].astype(f32).T
    return (
        result,
        tokens_grad,
        grad_qkv,
        grad_out,
        ffn_part[:, :ff].astype(f32),
        ffn_part[:, ff:].astype(f32).T,
        grad_norm[:2],
        grad_norm[2:],
    )


def solution(mesh):
    placed = (
        P("dp", "mp", None),
        P(None, "dp", "mp"),
        P("mp", "dp"),
        P("dp", "mp"),
        P("mp", "dp"),
        P(None, "dp"),
        P(None, "dp"),
        P("dp", None),
        P("dp", "mp", None),
    )
    return jax.shard_map(
        body,
        mesh=mesh,
        in_specs=placed,
        out_specs=(
            P("dp", "mp", None),
            P("dp", "mp", None),
            P(None, "dp", "mp"),
            P("mp", "dp"),
            P("dp", "mp"),
            P("mp", "dp"),
            P(None, "dp"),
            P(None, "dp"),
        ),
        check_vma=False,
    )
```
